128 devices in a mesh: blk: 8 (over x, y_hi), pts: 16 (over y_lo, z, core).
Axes of the slice: x: 4, y: 4 (y_hi: 2, y_lo: 2; y = y_hi * 2 + y_lo), z: 4, core: 2. Of those that a mesh axis runs over, the one named last changes fastest.
Arguments:
- point_feats: bfloat16 [1024, 128, 768], P(('blk', 'pts')), may hold values from -6 to 6
- point_pos: bfloat16 [1024, 3, 128], P(('blk', 'pts')), may hold values from 0 to 1
- anchor_pos: float32 [3, 2048], P(None, ('blk', 'pts')), may hold values from 0 to 1
- send_tiles: int32 [128, 16, 2], P(('blk', 'pts')), may hold values from 0 to 7
- nbr_slots: int32 [2048, 8], P(('blk', 'pts')), may hold values from 0 to 31
- nbr_counts: int32 [2048], P(('blk', 'pts')), may hold values from 1 to 8
- in_weight: bfloat16 [768, 768], replicated, may hold values from -0.21875 to 0.21875
- q_weight: bfloat16 [768, 768], replicated, may hold values from -3 to 3
- k_weight: bfloat16 [768, 768], replicated, may hold values from -3 to 3
- v_weight: bfloat16 [768, 768], replicated, may hold values from -0.21875 to 0.21875
- out_weight: bfloat16 [768, 768], replicated, may hold values from -0.21875 to 0.21875
- up_weight: bfloat16 [768, 3072], replicated, may hold values from -0.21875 to 0.21875
- down_weight: bfloat16 [3072, 768], replicated, may hold values from -0.109375 to 0.109375
Outputs:
- anchors_out: float32 [2048, 768], P(('blk', 'pts'))
- points_out: float32 [1024, 128, 768], P(('blk', 'pts'))
The draws below stay inside these ranges and needn't reach their ends.
Inputs may be any that keep to these rules, and one draw needn't show every extreme that they name: `send_tiles`: local tile numbers within the sending group; a tile may be named for several owners or twice. `nbr_slots`: slot numbers q * 2 + k of the tiles that the anchor's group receives; entries at positions from nbr_counts on are padding.
All inputs are finite; a program needn't handle non-finite values.
Results may differ from the reference program's by a relative error of at most 0.017.
Values may be sent and summed in bfloat16 or wider, within the bound.
A program may use at most 128 MiB of HBM per device.

```python
import math
import jax
import jax.numpy as jnp
from jax import lax

D = 768
HEADS = 12
HD = 64
FFH = 3072
A_DEV = 16
TILES_DEV = 8
TILE = 128
SEND_CAP = 2
NBR_CAP = 8
ANCHORS = 2048
TILES = 1024
N_BLK = 8
N_PTS = 16
DEVICES = 128


def draw_q_weight(key, part):
    jitter = jnp.clip(jax.random.normal(jax.random.fold_in(key, 201), (D, D), jnp.float32), -3.0, 3.0)
    return (1.8 * jitter / math.sqrt(D)).astype(jnp.bfloat16)


def draw_k_weight(key, part):
    jitter = jnp.clip(jax.random.normal(jax.random.fold_in(key, 301), (D, D), jnp.float32), -3.0, 3.0)
    return (1.8 * jitter / math.sqrt(D)).astype(jnp.bfloat16)


def place_ends(result, rng, low, largest):
    longest = result.shape.index(max(result.shape))
    spots = []
    for shift in (0, 1):
        where = [jax.random.randint(jax.random.fold_in(rng, axis), (), 0, length) for axis, length in enumerate(result.shape)]
        where[longest] = (where[longest] + shift) % result.shape[longest]
        spots.append(tuple(where))
    return result.at[spots[0]].set(low).at[spots[1]].set(largest)


def steps_of(rng, dims, shards, low, high):
    def one(position, shards_of):
        heights = jax.random.uniform(jax.random.fold_in(jax.random.fold_in(rng, 6), position), (shards_of,), jnp.float32, low / len(shards), high / len(shards))
        return jnp.repeat(jnp.exp(heights), dims[position] // shards_of).reshape((-1,) + (1,) * (len(dims) - position - 1))

    loudness = one(*shards[0])
    for cut in shards[1:]:
        loudness = loudness * one(*cut)
    return loudness


def scatter_about(rng, shape, scale, limit, cuts=(), kind=jnp.bfloat16):
    result = jax.random.normal(rng, shape, jnp.float32) * scale
    if len(cuts) > 0:
        result = steps_of(rng, shape, cuts, -0.22, 0.18) * result
    return jnp.clip(result, min=-limit, max=limit).astype(kind)


def setup_inputs(seed: int = 0) -> dict:
    arg_keys = jax.random.split(jax.random.key(seed), 14)
    return {
        "point_feats": scatter_about(arg_keys[0], (TILES, TILE, D), 1.0, 6.0, ((0, 128),)),
        "point_pos": jnp.clip(1.0 * jax.random.uniform(arg_keys[1], (TILES, 3, TILE), jnp.float32) ** steps_of(arg_keys[1], (TILES, 3, TILE), ((0, 128),), -0.2, 0.2), 0.0, 1.0).astype(jnp.bfloat16),
        "anchor_pos": jnp.clip(1.0 * jax.random.uniform(arg_keys[2], (3, ANCHORS), jnp.float32) ** steps_of(arg_keys[2], (3, ANCHORS), ((1, 128),), -0.2, 0.2), 0.0, 1.0),
        "send_tiles": place_ends(jax.random.randint(arg_keys[3], (DEVICES, N_PTS, SEND_CAP), 0, TILES_DEV), jax.random.fold_in(arg_keys[3], 1), 0, TILES_DEV - 1).astype(jnp.int32),
        "nbr_slots": place_ends(jax.random.randint(arg_keys[4], (ANCHORS, NBR_CAP), 0, N_PTS * SEND_CAP), jax.random.fold_in(arg_keys[4], 1), 0, (N_PTS * SEND_CAP) - 1).astype(jnp.int32),
        "nbr_counts": place_ends(jax.random.randint(arg_keys[5], (ANCHORS,), 1, NBR_CAP + 1), jax.random.fold_in(arg_keys[5], 1), 1, NBR_CAP).astype(jnp.int32),
        "in_weight": scatter_about(arg_keys[6], (D, D), D ** -0.5, 0.21875),
        "q_weight": draw_q_weight(jax.random.fold_in(arg_keys[13], 71), 0),
        "k_weight": draw_k_weight(jax.random.fold_in(arg_keys[13], 71), 0),
        "v_weight": scatter_about(arg_keys[9], (D, D), D ** -0.5, 0.21875),
        "out_weight": scatter_about(arg_keys[10], (D, D), D ** -0.5, 0.21875),
        "up_weight": scatter_about(arg_keys[11], (D, FFH), D ** -0.5, 0.21875),
        "down_weight": scatter_about(arg_keys[12], (FFH, D), FFH ** -0.5, 0.109375),
    }


RADIUS_SQUARED = 0.05
EPSILON = 1e-06

def rms_scaled(stream):
    return stream * lax.rsqrt(lax.optimization_barrier(jnp.mean(stream * stream, axis=-1, keepdims=True)) + EPSILON)

def pool_anchors(arrived, arrived_pos, centres, slot_lists, slot_counts):
    received = arrived.shape[0] * arrived.shape[1]
    tile_len = arrived.shape[2]
    arrived_rows = arrived.reshape(received * tile_len, arrived.shape[3])
    places = arrived_pos.astype(jnp.float32).reshape(received, 3, tile_len)
    offsets = places[None, :, :, :] - jnp.transpose(centres)[:, None, :, None]
    distance = lax.optimization_barrier(jnp.sum(offsets * offsets, axis=2))
    kernel = 1.0 / (1.0 + distance / RADIUS_SQUARED)
    positions = jnp.arange(slot_lists.shape[1], dtype=jnp.int32)
    in_list = positions[None, :] < slot_counts[:, None]
    matches = (slot_lists[:, :, None] == jnp.arange(received, dtype=jnp.int32)[None, None, :]) & in_list[:, :, None]
    picked = lax.optimization_barrier(jnp.sum(matches.astype(jnp.float32), axis=1))
    pool_weights = (picked[:, :, None] * kernel).reshape(centres.shape[1], received * tile_len).astype(jnp.bfloat16)
    summed = jnp.dot(pool_weights, arrived_rows, preferred_element_type=jnp.float32)
    return summed / slot_counts.astype(jnp.float32)[:, None]

def finish_stream(stream, attended, out_weight, up_weight, down_weight):
    residual = stream + jnp.dot(attended, out_weight, preferred_element_type=jnp.float32)
    normed = rms_scaled(residual).astype(jnp.bfloat16)
    hidden = jax.nn.gelu(jnp.dot(normed, up_weight, preferred_element_type=jnp.float32)).astype(jnp.bfloat16)
    return residual + jnp.dot(hidden, down_weight, preferred_element_type=jnp.float32)

def attend_all(queries, key_rows, value_rows):
    score_scale = 1.0 / math.sqrt(HD)
    scores = jnp.einsum('qhd,khd->hqk', queries.astype(jnp.float32), key_rows.astype(jnp.float32), precision=lax.Precision.HIGHEST) * score_scale
    row_max = lax.optimization_barrier(jnp.max(scores, axis=-1, keepdims=True))
    weights = jnp.exp(scores - row_max)
    totals = lax.optimization_barrier(jnp.sum(weights, axis=-1))
    rounded = weights.astype(jnp.bfloat16).astype(jnp.float32)
    attended = jnp.einsum('hqk,khd->qhd', rounded, value_rows.astype(jnp.float32), precision=lax.Precision.HIGHEST)
    return attended / jnp.transpose(totals)[:, :, None]

def take_tiles(sender_rows, indices):
    return jnp.take(sender_rows, indices, axis=0)

def reference(point_feats, point_pos, anchor_pos, send_tiles, nbr_slots, nbr_counts, in_weight, q_weight, k_weight, v_weight, out_weight, up_weight, down_weight):
    feature_width = point_feats.shape[2]
    embedded = jnp.dot(point_feats.reshape(TILES * TILE, feature_width), in_weight, preferred_element_type=jnp.float32).astype(jnp.bfloat16)
    grouped = embedded.reshape(N_BLK, N_PTS, TILES_DEV, TILE, feature_width)
    grouped_pos = point_pos.reshape(N_BLK, N_PTS, TILES_DEV, 3, TILE)
    send_lists = send_tiles.reshape(N_BLK, N_PTS, N_PTS, SEND_CAP)

    def pool_device(device):
        column = device // N_PTS
        within = device % N_PTS
        group_rows = lax.dynamic_index_in_dim(grouped, column, 0, keepdims=False)
        group_pos = lax.dynamic_index_in_dim(grouped_pos, column, 0, keepdims=False)
        group_lists = lax.dynamic_index_in_dim(send_lists, column, 0, keepdims=False)
        chosen = lax.dynamic_index_in_dim(group_lists, within, 1, keepdims=False)
        arrived = jax.vmap(take_tiles)(group_rows, chosen)
        arrived_pos = jax.vmap(take_tiles)(group_pos, chosen)
        centres = lax.dynamic_slice_in_dim(anchor_pos, device * A_DEV, A_DEV, 1)
        slot_lists = lax.dynamic_slice_in_dim(nbr_slots, device * A_DEV, A_DEV, 0)
        slot_counts = lax.dynamic_slice_in_dim(nbr_counts, device * A_DEV, A_DEV, 0)
        return pool_anchors(arrived, arrived_pos, centres, slot_lists, slot_counts)
    pooled = lax.map(pool_device, jnp.arange(DEVICES, dtype=jnp.int32))
    anchor_normed = rms_scaled(pooled.reshape(ANCHORS, feature_width)).astype(jnp.bfloat16)
    key_rows = jnp.dot(anchor_normed, k_weight, preferred_element_type=jnp.float32).astype(jnp.bfloat16).reshape(ANCHORS, HEADS, HD)
    value_rows = jnp.dot(anchor_normed, v_weight, preferred_element_type=jnp.float32).astype(jnp.bfloat16).reshape(ANCHORS, HEADS, HD)
    point_stream = embedded.astype(jnp.float32).reshape(DEVICES, TILES_DEV * TILE, feature_width)

    def finish_device(stacked):
        anchor_part, point_part = stacked
        stream = jnp.concatenate([anchor_part, point_part], axis=0)
        normed = rms_scaled(stream).astype(jnp.bfloat16)
        queries = jnp.dot(normed, q_weight, preferred_element_type=jnp.float32).astype(jnp.bfloat16).reshape(stream.shape[0], HEADS, HD)
        attended = attend_all(queries, key_rows, value_rows).reshape(stream.shape[0], feature_width).astype(jnp.bfloat16)
        return finish_stream(stream, attended, out_weight, up_weight, down_weight)
    finished = lax.map(finish_device, (pooled, point_stream))
    anchors_out = finished[:, :A_DEV, :].reshape(ANCHORS, feature_width)
    points_out = finished[:, A_DEV:, :].reshape(TILES, TILE, feature_width)
    return (anchors_out, points_out)
```

```python
import jax, jax.numpy as jnp
from jax import lax
from jax.experimental import pallas as pl
from jax.experimental.pallas import tpu as pltpu
from jax.sharding import PartitionSpec as P

HEADS=12; HD=64; D=768; FFH=3072; A=2048
ROWS=208; EPS=1e-6
LOG2E=1.4426950408889634

def rms(x):
    return x*lax.rsqrt(jnp.mean(x*x,axis=-1,keepdims=True)+EPS)

def dot(a,b):
    return jnp.dot(a,b,preferred_element_type=jnp.float32)

def kern(emb, pooled, nrm, wq_h, wk_h, wv_h, wo_h, wu_h, wd_h, anc_out, pts_out,
         wq, wk, wv, wo, wu, wd, kt, va, xs, osc, att, sems, osem):
    i=pl.program_id(0); n=pl.num_programs(0)
    pairs=((wk_h,wk),(wv_h,wv),(wq_h,wq),(wo_h,wo),(wu_h,wu),(wd_h,wd))
    def cp(j):
        return pltpu.make_async_copy(pairs[j][0],pairs[j][1],sems.at[j])
    def ocopy(j,slot):
        return pltpu.make_async_copy(osc.at[slot],pts_out.at[pl.ds(j*ROWS,ROWS)],osem.at[slot])
    @pl.when(i==0)
    def _():
        for j in range(6): cp(j).start()
        cp(0).wait()
        lane=lax.broadcasted_iota(jnp.int32,(256,128),1)
        lo=lane<HD
        wkT=wk[...].T
        for c in range(0,A,256):
            acc=None
            acv=None
            for part in range(3):
                blk=nrm[c:c+256,part*256:part*256+256]
                t=lax.dot_general(wkT[:,part*256:part*256+256],blk,(((1,),(1,)),((),())),preferred_element_type=jnp.float32)
                acc=t if acc is None else acc+t
            kt[:,c:c+256]=acc.astype(jnp.bfloat16)
        cp(1).wait()
        one=jnp.ones((256,128),jnp.bfloat16); zero=jnp.zeros((256,128),jnp.bfloat16)
        for c in range(0,A,256):
            acv=None
            for part in range(3):
                blk=nrm[c:c+256,part*256:part*256+256]
                t=dot(blk,wv[part*256:part*256+256,:])
                acv=t if acv is None else acv+t
            v=acv.astype(jnp.bfloat16)
            for p in range(HEADS//2):
                vp=v[:,128*p:128*p+128]
                va[2*p,c:c+256,0:128]=jnp.where(lo,vp,zero)
                va[2*p,c:c+256,128:256]=jnp.where(lo,one,zero)
                va[2*p+1,c:c+256,0:128]=jnp.where(lo,zero,vp)
                va[2*p+1,c:c+256,128:256]=jnp.where(lo,zero,one)
        cp(2).wait(); cp(3).wait()
    @pl.when(i<n-1)
    def _():
        xs[...]=emb[pl.ds(pl.multiple_of(i*ROWS,16),ROWS),:].astype(jnp.float32)
    @pl.when(i==n-1)
    def _():
        xs[0:ROWS-16,:]=emb[1024-(ROWS-16):1024,:].astype(jnp.float32)
        xs[ROWS-16:ROWS,:]=pooled[...]
    x=xs[...]
    nx=rms(x).astype(jnp.bfloat16)
    q=(dot(nx,wq[...])*(LOG2E/8.0)).astype(jnp.bfloat16)
    lane=lax.broadcasted_iota(jnp.int32,(ROWS,128),1)
    lo=lane<HD
    for p in range(HEADS//2):
        qp=q[:,128*p:128*p+128]
        zero=jnp.zeros_like(qp)
        o=jnp.zeros((ROWS,256),jnp.float32)
        for a in range(2):
            qa=jnp.where(lo,qp,zero) if a==0 else jnp.where(lo,zero,qp)
            s=dot(qa,kt[128*p:128*p+128,:])
            m=jnp.max(s,axis=1,keepdims=True)
            w=jnp.exp2(s-m).astype(jnp.bfloat16)
            o=o+dot(w,va[2*p+a,:,:])
        att[:,128*p:128*p+128]=(o[:,0:128]/o[:,128:256]).astype(jnp.bfloat16)
    res=x+dot(att[...],wo[...])
    @pl.when(i==0)
    def _():
        cp(4).wait(); cp(5).wait()
    n2=rms(res).astype(jnp.bfloat16)
    FC=768
    acc=res
    for c in range(0,FFH,FC):
        h=jax.nn.gelu(dot(n2,wu[:,c:c+FC])).astype(jnp.bfloat16)
        acc=acc+dot(h,wd[c:c+FC,:])
    slot=lax.rem(i,2)
    @pl.when(i>=2)
    def _():
        ocopy(i-2,slot).wait()
    osc[slot]=acc
    @pl.when(i<n-1)
    def _():
        ocopy(i,slot).start()
    @pl.when(i==n-1)
    def _():
        c1=pltpu.make_async_copy(osc.at[slot,pl.ds(0,ROWS-16)],pts_out.at[pl.ds(1024-(ROWS-16),ROWS-16)],osem.at[2])
        c2=pltpu.make_async_copy(osc.at[slot,pl.ds(ROWS-16,16)],anc_out,osem.at[3])
        c1.start(); c2.start()
        ocopy(i-1,1-slot).wait()
        c1.wait(); c2.wait()

def compute(emb,pooled,nrm,wq,wk,wv,wo,wu,wd):
    n=1040//ROWS
    full=pl.BlockSpec(memory_space=pltpu.VMEM)
    anys=pl.BlockSpec(memory_space=pl.ANY)
    bf=jnp.bfloat16
    return pl.pallas_call(kern,grid=(n,),
      in_specs=[full,full,full]+[anys]*6, out_specs=[anys,anys],
      out_shape=[jax.ShapeDtypeStruct((16,D),jnp.float32),jax.ShapeDtypeStruct((1024,D),jnp.float32)],
      scratch_shapes=[pltpu.VMEM((D,D),bf)]*4+[pltpu.VMEM((D,FFH),bf),pltpu.VMEM((FFH,D),bf),
        pltpu.VMEM((D,A),bf),pltpu.VMEM((HEADS,A,256),bf),pltpu.VMEM((ROWS,D),jnp.float32),pltpu.VMEM((2,ROWS,D),jnp.float32),
        pltpu.VMEM((ROWS,D),bf),pltpu.SemaphoreType.DMA((6,)),pltpu.SemaphoreType.DMA((4,))],
      compiler_params=pltpu.CompilerParams(vmem_limit_bytes=60*2**20,dimension_semantics=("arbitrary",)),
    )(emb,pooled,nrm,wq,wk,wv,wo,wu,wd)


def body(point_feats, point_pos, anchor_pos, send_tiles, nbr_slots, nbr_counts, in_weight, q_weight, k_weight, v_weight,
         out_weight, up_weight, down_weight):
    feats = point_feats.reshape(1024, D)
    me = lax.axis_index("pts")
    counts = nbr_counts.astype(jnp.float32)
    info = jnp.concatenate([anchor_pos.T, counts[:, None], nbr_slots.astype(jnp.float32)], axis=1)
    info = lax.all_gather(info, "pts", axis=0, tiled=True)
    emb = dot(feats, in_weight).astype(jnp.bfloat16)
    slots = info[:, 4:12]
    live = jnp.arange(8, dtype=jnp.float32)[None, :] < info[:, 3:4]
    base = (2 * me).astype(jnp.float32)
    sent = jnp.repeat(send_tiles[0], 16, axis=0)
    tiles = jnp.arange(8, dtype=jnp.int32)[None, :]
    counted = 0.0
    for k in range(2):
        times = jnp.sum(((slots == base + k) & live).astype(jnp.float32), axis=1, keepdims=True)
        counted = counted + jnp.where(sent[:, k:k + 1] == tiles, times, 0.0)
    places = point_pos.astype(jnp.float32)
    offsets = places[None] - info[:, None, 0:3, None]
    distance = jnp.sum(offsets * offsets, axis=2)
    weights = (counted[:, :, None] / (1.0 + distance / 0.05)).reshape(256, 1024).astype(jnp.bfloat16)
    partial = dot(weights, emb).astype(jnp.bfloat16)
    arrived = lax.all_to_all(partial.reshape(16, 16, D), "pts", split_axis=0, concat_axis=0, tiled=True)
    pooled = jnp.sum(arrived.astype(jnp.float32), axis=0) / counts[:, None]
    normed = rms(pooled).astype(jnp.bfloat16)
    gathered = lax.all_gather(normed, ("blk", "pts"), axis=0, tiled=True)
    anchors, points = compute(emb, pooled, gathered, q_weight, k_weight, v_weight, out_weight, up_weight, down_weight)
    return anchors, points.reshape(8, 128, D)


def solution(mesh):
    both = ("blk", "pts")
    return jax.shard_map(
        body,
        mesh=mesh,
        in_specs=(P(both, None, None), P(both, None, None), P(None, both), P(both, None, None), P(both, None), P(both))
        + (P(),) * 7,
        out_specs=(P(both, None), P(both, None, None)),
        check_vma=False,
    )
```

```python
import jax, jax.numpy as jnp
from jax import lax
from jax.experimental import pallas as pl
from jax.experimental.pallas import tpu as pltpu
from jax.sharding import PartitionSpec as P

HEADS=12; HD=64; D=768; FFH=3072; A=2048
ROWS=208; EPS=1e-6
LOG2E=1.4426950408889634

def rms(x):
    return x*lax.rsqrt(jnp.mean(x*x,axis=-1,keepdims=True)+EPS)

def dot(a,b):
    return jnp.dot(a,b,preferred_element_type=jnp.float32)

def kern(emb, pooled, nrm, wq_h, wk_h, wv_h, wo_h, wu_h, wd_h, anc_out, pts_out,
         wq, wk, wv, wo, wu, wd, kt, va, xs, osc, att, sems, osem):
    i=pl.program_id(0); n=pl.num_programs(0)
    pairs=((wk_h,wk),(wv_h,wv),(wq_h,wq),(wo_h,wo),(wu_h,wu),(wd_h,wd))
    def cp(j):
        return pltpu.make_async_copy(pairs[j][0],pairs[j][1],sems.at[j])
    def ocopy(j,slot):
        return pltpu.make_async_copy(osc.at[slot],pts_out.at[pl.ds(j*ROWS,ROWS)],osem.at[slot])
    @pl.when(i==0)
    def _():
        for j in range(6): cp(j).start()
        cp(0).wait()
        lane=lax.broadcasted_iota(jnp.int32,(256,128),1)
        lo=lane<HD
        wkT=wk[...].T
        for c in range(0,A,256):
            acc=None
            acv=None
            for part in range(3):
                blk=nrm[part,c:c+256,:]
                t=lax.dot_general(wkT[:,part*256:part*256+256],blk,(((1,),(1,)),((),())),preferred_element_type=jnp.float32)
                acc=t if acc is None else acc+t
            kt[:,c:c+256]=acc.astype(jnp.bfloat16)
        cp(1).wait()
        one=jnp.ones((256,128),jnp.bfloat16); zero=jnp.zeros((256,128),jnp.bfloat16)
        for c in range(0,A,256):
            acv=None
            for part in range(3):
                blk=nrm[part,c:c+256,:]
                t=dot(blk,wv[part*256:part*256+256,:])
                acv=t if acv is None else acv+t
            v=acv.astype(jnp.bfloat16)
            for p in range(HEADS//2):
                vp=v[:,128*p:128*p+128]
                va[2*p,c:c+256,0:128]=jnp.where(lo,vp,zero)
                va[2*p,c:c+256,128:256]=jnp.where(lo,one,zero)
                va[2*p+1,c:c+256,0:128]=jnp.where(lo,zero,vp)
                va[2*p+1,c:c+256,128:256]=jnp.where(lo,zero,one)
        cp(2).wait(); cp(3).wait()
    @pl.when(i<n-1)
    def _():
        xs[...]=emb[pl.ds(pl.multiple_of(i*ROWS,16),ROWS),:].astype(jnp.float32)
    @pl.when(i==n-1)
    def _():
        xs[0:ROWS-16,:]=emb[1024-(ROWS-16):1024,:].astype(jnp.float32)
        xs[ROWS-16:ROWS,:]=pooled[...]
    x=xs[...]
    nx=rms(x).astype(jnp.bfloat16)
    q=(dot(nx,wq[...])*(LOG2E/8.0)).astype(jnp.bfloat16)
    lane=lax.broadcasted_iota(jnp.int32,(ROWS,128),1)
    lo=lane<HD
    for p in range(HEADS//2):
        qp=q[:,128*p:128*p+128]
        zero=jnp.zeros_like(qp)
        o=jnp.zeros((ROWS,256),jnp.float32)
        for a in range(2):
            qa=jnp.where(lo,qp,zero) if a==0 else jnp.where(lo,zero,qp)
            s=dot(qa,kt[128*p:128*p+128,:])
            m=jnp.max(s,axis=1,keepdims=True)
            w=jnp.exp2(s-m).astype(jnp.bfloat16)
            o=o+dot(w,va[2*p+a,:,:])
        att[:,128*p:128*p+128]=(o[:,0:128]/o[:,128:256]).astype(jnp.bfloat16)
    res=x+dot(att[...],wo[...])
    @pl.when(i==0)
    def _():
        cp(4).wait(); cp(5).wait()
    n2=rms(res).astype(jnp.bfloat16)
    FC=768
    acc=res
    for c in range(0,FFH,FC):
        h=jax.nn.gelu(dot(n2,wu[:,c:c+FC])).astype(jnp.bfloat16)
        acc=acc+dot(h,wd[c:c+FC,:])
    slot=lax.rem(i,2)
    @pl.when(i>=2)
    def _():
        ocopy(i-2,slot).wait()
    osc[slot]=acc
    @pl.when(i<n-1)
    def _():
        ocopy(i,slot).start()
    @pl.when(i==n-1)
    def _():
        c1=pltpu.make_async_copy(osc.at[slot,pl.ds(0,ROWS-16)],pts_out.at[pl.ds(1024-(ROWS-16),ROWS-16)],osem.at[2])
        c2=pltpu.make_async_copy(osc.at[slot,pl.ds(ROWS-16,16)],anc_out,osem.at[3])
        c1.start(); c2.start()
        ocopy(i-1,1-slot).wait()
        c1.wait(); c2.wait()

def compute(emb,pooled,nrm,wq,wk,wv,wo,wu,wd):
    n=1040//ROWS
    full=pl.BlockSpec(memory_space=pltpu.VMEM)
    anys=pl.BlockSpec(memory_space=pl.ANY)
    bf=jnp.bfloat16
    return pl.pallas_call(kern,grid=(n,),
      in_specs=[full,full,full]+[anys]*6, out_specs=[anys,anys],
      out_shape=[jax.ShapeDtypeStruct((16,D),jnp.float32),jax.ShapeDtypeStruct((1024,D),jnp.float32)],
      scratch_shapes=[pltpu.VMEM((D,D),bf)]*4+[pltpu.VMEM((D,FFH),bf),pltpu.VMEM((FFH,D),bf),
        pltpu.VMEM((D,A),bf),pltpu.VMEM((HEADS,A,256),bf),pltpu.VMEM((ROWS,D),jnp.float32),pltpu.VMEM((2,ROWS,D),jnp.float32),
        pltpu.VMEM((ROWS,D),bf),pltpu.SemaphoreType.DMA((6,)),pltpu.SemaphoreType.DMA((4,))],
      compiler_params=pltpu.CompilerParams(vmem_limit_bytes=60*2**20,dimension_semantics=("arbitrary",)),
    )(emb,pooled,nrm,wq,wk,wv,wo,wu,wd)


CORES = 2
RING = 4
GROUP = 16


def gather_kernel(
    feats_hbm, win_hbm, pos_ref, apos_ref, send_ref, slots_ref, counts_ref,
    emb_ref, pooled_ref, box_ref,
    feats, win, flip, info, pweights, outgoing, incoming,
    local_sem, info_send, info_recv, part_send, part_recv, box_send, box_recv, twin_send, twin_recv,
):
    blk = lax.axis_index("blk")
    pts = lax.axis_index("pts")
    x, y_hi = blk // 2, lax.rem(blk, 2)
    core = lax.rem(pts, 2)
    chip = pts // 2
    z, y_lo = lax.rem(chip, 4), chip // 4
    y = y_hi * 2 + y_lo
    place = (x, y, z)

    def device(spot, c):
        return (spot[0] * 2 + spot[1] // 2, (lax.rem(spot[1], 2) * 4 + spot[2]) * 2 + c)

    def ring(axis, step):
        spot = list(place)
        spot[axis] = lax.rem(place[axis] + step, RING)
        return tuple(spot)

    def mate(step):
        return lax.rem(pts + step, GROUP)

    load_feats = pltpu.make_async_copy(feats_hbm, feats, local_sem.at[0])
    load_win = pltpu.make_async_copy(win_hbm, win, local_sem.at[1])
    load_win.start()
    load_feats.start()

    barrier = pltpu.get_barrier_semaphore()

    def greet(device_id):
        pl.semaphore_signal(barrier, inc=1, device_id=device_id, device_id_type=pl.DeviceIdType.MESH)

    for step in range(1, GROUP):
        greet((blk, mate(step)))
    for step in range(1, RING):
        greet(device(ring(0, step), core))
    across = lax.rem(y_hi + 1, 2)
    for low in range(2):
        greet((x * 2 + across, (low * 4 + z) * 2 + core))

    flip[...] = jnp.zeros_like(flip)
    flip[0:3, 0:16] = apos_ref[...]
    flip[3:4, 0:16] = counts_ref[...].astype(jnp.float32)
    flip[8:16, 0:16] = slots_ref[...].astype(jnp.float32)
    turned = flip[...].T
    info[pl.ds(pts, 1)] = turned[0:16, :][None]
    pl.semaphore_wait(barrier, 20)

    def send_info(step):
        return pltpu.make_async_remote_copy(
            src_ref=info.at[pts], dst_ref=info.at[pts], send_sem=info_send.at[step - 1], recv_sem=info_recv.at[step - 1],
            device_id=(blk, mate(step)), device_id_type=pl.DeviceIdType.MESH,
        )

    for step in range(1, GROUP):
        send_info(step).start()
    load_win.wait()
    load_feats.wait()
    for rows in range(0, 1024, 256):
        emb_ref[rows:rows + 256, :] = dot(feats[rows:rows + 256, :], win[...]).astype(jnp.bfloat16)
    for step in range(1, GROUP):
        send_info(step).wait()

    lane = lax.broadcasted_iota(jnp.int32, (16, 128), 1)
    for p in range(GROUP):
        facts = info[p]
        count = facts[:, 3:4]
        listed = (lane >= 8) & (lane < 16) & ((lane - 8).astype(jnp.float32) < count)
        times = []
        for k in range(2):
            hit = listed & (facts.astype(jnp.int32) == 2 * pts + k)
            times.append(jnp.sum(jnp.where(hit, 1.0, 0.0), axis=1, keepdims=True) + jnp.zeros((16, 128), jnp.float32))
        named = [send_ref[k:k + 1, p:p + 1] + jnp.zeros((16, 128), jnp.int32) for k in range(2)]
        centre = [facts[:, n:n + 1] + jnp.zeros((16, 128), jnp.float32) for n in range(3)]
        for t in range(8):
            distance = 0.0
            for n in range(3):
                offset = pos_ref[n, t:t + 1, :].astype(jnp.float32) - centre[n]
                distance = distance + offset * offset
            often = jnp.where(named[0] == t, times[0], 0.0) + jnp.where(named[1] == t, times[1], 0.0)
            pweights[16 * p:16 * p + 16, 128 * t:128 * t + 128] = (often / (1.0 + distance / 0.05)).astype(jnp.bfloat16)

    outgoing[...] = dot(pweights[...], emb_ref[...]).astype(jnp.bfloat16).reshape(outgoing.shape)

    def send_part(step):
        return pltpu.make_async_remote_copy(
            src_ref=outgoing.at[mate(step)], dst_ref=incoming.at[pts], send_sem=part_send.at[step - 1],
            recv_sem=part_recv.at[step - 1], device_id=(blk, mate(step)), device_id_type=pl.DeviceIdType.MESH,
        )

    for step in range(1, GROUP):
        send_part(step).start()
    incoming[pl.ds(pts, 1)] = outgoing[pl.ds(pts, 1)]
    for step in range(1, GROUP):
        send_part(step).wait()
    total = incoming[0].astype(jnp.float32)
    for p in range(1, GROUP):
        total = total + incoming[p].astype(jnp.float32)
    pooled = total / turned[0:16, 3:4]
    pooled_ref[...] = pooled
    normed = rms(pooled).astype(jnp.bfloat16)
    for part in range(3):
        box_ref[part, x, y, z, core] = normed[:, 256 * part:256 * part + 256]

    def box(part, spot, stage):
        where = list(spot)
        for earlier in range(stage):
            where[(part + earlier) % 3] = slice(None)
        return tuple(where)

    def send_box(part, stage, step):
        axis = (part + stage) % 3
        view = box_ref.at[(part,) + box(part, place, stage) + (core,)]
        return pltpu.make_async_remote_copy(
            src_ref=view, dst_ref=view, send_sem=box_send.at[part, stage, step - 1], recv_sem=box_recv.at[part, stage, step - 1],
            device_id=device(ring(axis, step), core), device_id_type=pl.DeviceIdType.MESH,
        )

    def send_twin(part, stage, step):
        if stage == 0:
            where, slot = box(part, place, 1), 0
        else:
            axis = (part + stage) % 3
            where, slot = box(part, ring(axis, RING - step), stage), 3 * stage - 3 + step
        view = box_ref.at[(part,) + where + (core,)]
        return pltpu.make_async_remote_copy(
            src_ref=view, dst_ref=view, send_sem=twin_send.at[part, slot], recv_sem=twin_recv.at[part, slot],
            device_id=(blk, chip * 2 + 1 - core), device_id_type=pl.DeviceIdType.MESH,
        )

    order = (1, 3, 2)
    for part in range(3):
        for step in order:
            send_box(part, 0, step).start()
    for stage in range(1, 3):
        for part in range(3):
            for step in order:
                send_box(part, stage - 1, step).wait_recv()
            for step in order:
                send_box(part, stage, step).start()
            if stage == 1:
                send_twin(part, 0, 0).start()
            else:
                for step in order:
                    send_twin(part, 1, step).start()
    for step in order:
        for part in range(3):
            send_box(part, 2, step).wait_recv()
            send_twin(part, 2, step).start()
    for part in range(3):
        send_twin(part, 0, 0).wait()
        for stage in range(3):
            for step in order:
                send_box(part, stage, step).wait_send()
                if stage > 0:
                    send_twin(part, stage, step).wait()


def gather(feats, in_weight, point_pos, anchor_pos, send_tiles, nbr_slots, nbr_counts):
    vmem = pl.BlockSpec(memory_space=pltpu.VMEM)
    anywhere = pl.BlockSpec(memory_space=pl.ANY)
    bf = jnp.bfloat16
    dma = pltpu.SemaphoreType.DMA
    return pl.pallas_call(
        gather_kernel,
        in_specs=[anywhere] * 2 + [vmem] * 5,
        out_specs=[vmem] * 3,
        out_shape=[
            jax.ShapeDtypeStruct((1024, D), bf),
            jax.ShapeDtypeStruct((16, D), jnp.float32),
            jax.ShapeDtypeStruct((3, RING, RING, RING, CORES, 16, 256), bf),
        ],
        scratch_shapes=[
            pltpu.VMEM((1024, D), bf), pltpu.VMEM((D, D), bf), pltpu.VMEM((128, 128), jnp.float32),
            pltpu.VMEM((GROUP, 16, 128), jnp.float32), pltpu.VMEM((256, 1024), bf), pltpu.VMEM((GROUP, 16, D), bf),
            pltpu.VMEM((GROUP, 16, D), bf), dma((2,)), dma((15,)), dma((15,)), dma((15,)), dma((15,)),
            dma((3, 3, 3)), dma((3, 3, 3)), dma((3, 7)), dma((3, 7)),
        ],
        compiler_params=pltpu.CompilerParams(collective_id=0, has_side_effects=True, vmem_limit_bytes=40 * 2**20),
    )(feats, in_weight, point_pos, anchor_pos, send_tiles, nbr_slots, nbr_counts)


def body(point_feats, point_pos, anchor_pos, send_tiles, nbr_slots, nbr_counts, in_weight, q_weight, k_weight, v_weight,
         out_weight, up_weight, down_weight):
    emb, pooled, boxes = gather(
        point_feats.reshape(1024, D), in_weight, jnp.transpose(point_pos, (1, 0, 2)), anchor_pos, send_tiles[0].T, nbr_slots.T,
        nbr_counts[None],
    )
    anchors, points = compute(
        emb, pooled, boxes.reshape(3, A, 256), q_weight, k_weight, v_weight, out_weight, up_weight, down_weight
    )
    return anchors, points.reshape(8, 128, D)


def solution(mesh):
    both = ("blk", "pts")
    return jax.shard_map(
        body,
        mesh=mesh,
        in_specs=(P(both, None, None), P(both, None, None), P(None, both), P(both, None, None), P(both, None), P(both))
        + (P(),) * 7,
        out_specs=(P(both, None), P(both, None, None)),
        check_vma=False,
    )
```

```python
import jax
import jax.numpy as jnp
from jax import lax
from jax.experimental import pallas as pl
from jax.experimental.pallas import tpu as pltpu
from jax.sharding import PartitionSpec as P

HEADS = 12
HD = 64
D = 768
FFH = 3072
A = 2048
POINTS = 1024
ROWS = 208
EPS = 1e-6
LOG2E = 1.4426950408889634
CORES = 2
RING = 4
GROUP = 16
MESH = pl.DeviceIdType.MESH
BF = jnp.bfloat16
F32 = jnp.float32
MATES = [(1, 2, 0), (1, 2, 1), (1, 1, 0), (1, 3, 0), (1, 1, 1), (1, 3, 1), (0, 2, 0), (0, 2, 1),
         (1, 0, 0), (1, 0, 1), (0, 1, 0), (0, 3, 0), (0, 1, 1), (0, 3, 1), (0, 0, 1)]


def rms(rows):
    return rows * lax.rsqrt(jnp.mean(rows * rows, axis=-1, keepdims=True) + EPS)


def dot(left, right):
    return jnp.dot(left, right, preferred_element_type=F32)


def queries_of(rows, weight):
    return (dot(rms(rows).astype(BF), weight) * (LOG2E / 8.0)).astype(BF)


def gather_kernel(
    feats_hbm, win_hbm, wq_hbm, wk_hbm, wv_hbm, pos_hbm, apos_hbm, send_hbm, slots_hbm, counts_hbm,
    emb_ref, pooled_ref, q_ref, kt_ref, v_ref,
    feats, win, wq, wk, wv, pos_ref, apos_ref, send_ref, slots_ref, counts_ref,
    turn, info, pweights, outgoing, incoming, box_ref,
    local_sem, info_send, info_recv, part_send, part_recv,
    line_send, line_recv, plane_send, plane_recv, cube_send, cube_recv, twin_send, twin_recv,
):
    blk = lax.axis_index("blk")
    pts = lax.axis_index("pts")
    x, y_hi = blk // 2, lax.rem(blk, 2)
    core = lax.rem(pts, 2)
    chip = pts // 2
    z, y_lo = lax.rem(chip, 4), chip // 4
    y = y_hi * 2 + y_lo
    place = (x, y, z)

    def device(spot):
        return (spot[0] * 2 + spot[1] // 2, (lax.rem(spot[1], 2) * 4 + spot[2]) * 2 + core)

    def ring(axis, step):
        spot = list(place)
        spot[axis] = lax.rem(place[axis] + step, RING)
        return tuple(spot)

    def mate(n):
        dy, dz, dc = MATES[n]
        return (lax.rem(y_lo + dy, 2) * 4 + lax.rem(z + dz, RING)) * 2 + lax.rem(core + dc, 2)

    loads = [
        pltpu.make_async_copy(source, target, local_sem.at[n])
        for n, (source, target) in enumerate((
            (feats_hbm, feats), (win_hbm, win), (apos_hbm, apos_ref), (slots_hbm, slots_ref), (counts_hbm, counts_ref),
            (wq_hbm, wq), (send_hbm, send_ref), (pos_hbm, pos_ref), (wk_hbm, wk), (wv_hbm, wv)))
    ]
    for load in loads:
        load.start()

    barrier = pltpu.get_barrier_semaphore()

    def greet(device_id):
        pl.semaphore_signal(barrier, inc=1, device_id=device_id, device_id_type=MESH)

    for n in range(GROUP - 1):
        greet((blk, mate(n)))
    for step in range(1, RING):
        greet(device(ring(0, step)))
    across = lax.rem(y_hi + 1, 2)
    for low in range(2):
        greet((x * 2 + across, (low * 4 + z) * 2 + core))

    for n in range(2, 5):
        loads[n].wait()
    turn[...] = jnp.zeros_like(turn)
    turn[0:3, 0:16] = apos_ref[...]
    turn[3:4, 0:16] = counts_ref[...].astype(F32)
    turn[8:16, 0:16] = slots_ref[...].astype(F32)
    turned = turn[...].T[0:16, :]
    info[pl.ds(pts, 1)] = turned[None]
    loads[0].wait()
    loads[1].wait()
    for rows in range(0, POINTS, 256):
        emb_ref[rows:rows + 256, :] = dot(feats[rows:rows + 256, :], win[...]).astype(BF)

    pl.semaphore_wait(barrier, 20)

    def send_info(n):
        return pltpu.make_async_remote_copy(
            src_ref=info.at[pts], dst_ref=info.at[pts], send_sem=info_send.at[n], recv_sem=info_recv.at[n],
            device_id=(blk, mate(n)), device_id_type=MESH,
        )

    for n in range(GROUP - 1):
        send_info(n).start()
    for n in range(5, 8):
        loads[n].wait()
    for rows in range(0, POINTS, 256):
        q_ref[rows:rows + 256, :] = queries_of(emb_ref[rows:rows + 256, :].astype(F32), wq[...])
    for n in range(GROUP - 1):
        send_info(n).wait()

    lane = lax.broadcasted_iota(jnp.int32, (16, 128), 1)
    for p in range(GROUP):
        facts = info[p]
        count = facts[:, 3:4]
        listed = (lane >= 8) & (lane < 16) & ((lane - 8).astype(F32) < count)
        times = []
        for k in range(2):
            hit = listed & (facts.astype(jnp.int32) == 2 * pts + k)
            times.append(jnp.sum(jnp.where(hit, 1.0, 0.0), axis=1, keepdims=True) + jnp.zeros((16, 128), F32))
        named = [send_ref[k:k + 1, p:p + 1] + jnp.zeros((16, 128), jnp.int32) for k in range(2)]
        centre = [facts[:, n:n + 1] + jnp.zeros((16, 128), F32) for n in range(3)]
        for t in range(8):
            distance = 0.0
            for n in range(3):
                offset = pos_ref[n, t:t + 1, :].astype(F32) - centre[n]
                distance = distance + offset * offset
            often = jnp.where(named[0] == t, times[0], 0.0) + jnp.where(named[1] == t, times[1], 0.0)
            pweights[16 * p:16 * p + 16, 128 * t:128 * t + 128] = (often / (1.0 + distance / 0.05)).astype(BF)

    outgoing[...] = dot(pweights[...], emb_ref[...]).astype(BF).reshape(outgoing.shape)

    def send_part(n):
        return pltpu.make_async_remote_copy(
            src_ref=outgoing.at[mate(n)], dst_ref=incoming.at[pts], send_sem=part_send.at[n], recv_sem=part_recv.at[n],
            device_id=(blk, mate(n)), device_id_type=MESH,
        )

    for n in range(GROUP - 1):
        send_part(n).start()
    incoming[pl.ds(pts, 1)] = outgoing[pl.ds(pts, 1)]
    loads[8].wait()
    loads[9].wait()
    wk[...] = wk[...].T
    for n in range(GROUP - 1):
        send_part(n).wait()
    total = incoming[0].astype(F32)
    for p in range(1, GROUP):
        total = total + incoming[p].astype(F32)
    pooled = total / turned[:, 3:4]
    normed = rms(pooled).astype(BF)
    for part in range(3):
        box_ref[part, core, x, y, z] = normed[:, 256 * part:256 * part + 256]

    def axis_of(part, stage):
        return (part + stage) % 3

    def view(part, spot, free):
        where = list(spot)
        for stage in range(free):
            where[axis_of(part, stage)] = slice(None)
        return box_ref.at[(part, core) + tuple(where)]

    def send_line(part, step):
        block = view(part, place, 0)
        return pltpu.make_async_remote_copy(
            src_ref=block, dst_ref=block, send_sem=line_send.at[part, step], recv_sem=line_recv.at[part, step],
            device_id=device(ring(axis_of(part, 0), step)), device_id_type=MESH,
        )

    def send_plane(part, step):
        line = view(part, place, 1)
        return pltpu.make_async_remote_copy(
            src_ref=line, dst_ref=line, send_sem=plane_send.at[part, step], recv_sem=plane_recv.at[part, step],
            device_id=device(ring(axis_of(part, 1), step)), device_id_type=MESH,
        )

    def send_cube(part, piece, step):
        line = view(part, ring(axis_of(part, 1), (RING - piece) % RING), 1)
        return pltpu.make_async_remote_copy(
            src_ref=line, dst_ref=line, send_sem=cube_send.at[part, piece, step], recv_sem=cube_recv.at[part, piece, step],
            device_id=device(ring(axis_of(part, 2), step)), device_id_type=MESH,
        )

    def send_twin(part, slot):
        if slot < 4:
            block = view(part, ring(axis_of(part, 1), (RING - slot) % RING), 1)
        else:
            block = view(part, ring(axis_of(part, 2), RING + 3 - slot), 2)
        return pltpu.make_async_remote_copy(
            src_ref=block, dst_ref=block, send_sem=twin_send.at[part, slot], recv_sem=twin_recv.at[part, slot],
            device_id=(blk, chip * 2 + 1 - core), device_id_type=MESH,
        )

    steps = (2, 1, 3)
    for part in range(3):
        for step in steps:
            send_line(part, step).start()
    pooled_ref[...] = pooled
    q_ref[POINTS:POINTS + 16, :] = queries_of(pooled, wq[...])
    for part in range(3):
        for step in (1, 3, 2):
            send_line(part, step).wait_recv()
        for step in steps:
            send_plane(part, step).start()
        for step in steps:
            send_cube(part, 0, step).start()
        send_twin(part, 0).start()
    for piece in (1, 3, 2):
        for part in range(3):
            send_plane(part, piece).wait_recv()
            for step in steps:
                send_cube(part, piece, step).start()
            send_twin(part, piece).start()
    for step in (1, 3, 2):
        for part in range(3):
            for piece in (0, 1, 3, 2):
                send_cube(part, piece, step).wait_recv()
            send_twin(part, 3 + step).start()

    def project(half, first):
        blocks = [box_ref[part, half].reshape(A // 2, 256) for part in range(3)]
        for c in range(0, A // 2, 256):
            keys = None
            values = None
            for part in range(3):
                block = blocks[part][c:c + 256]
                columns = slice(256 * part, 256 * part + 256)
                key = lax.dot_general(wk[:, columns], block, (((1,), (1,)), ((), ())), preferred_element_type=F32)
                value = dot(block, wv[columns, :])
                keys = key if keys is None else keys + key
                values = value if values is None else values + value
            kt_ref[:, first + c:first + c + 256] = keys.astype(BF)
            v_ref[first + c:first + c + 256, :] = values.astype(BF)

    project(core, 0)
    for part in range(3):
        for slot in range(7):
            send_twin(part, slot).wait()
    project(1 - core, A // 2)
    for part in range(3):
        for step in steps:
            send_line(part, step).wait_send()
            send_plane(part, step).wait_send()
            for piece in range(RING):
                send_cube(part, piece, step).wait_send()


def gather(feats, in_weight, q_weight, k_weight, v_weight, point_pos, anchor_pos, send_tiles, nbr_slots, nbr_counts):
    vmem = pl.BlockSpec(memory_space=pltpu.VMEM)
    hbm = pl.BlockSpec(memory_space=pltpu.HBM)
    dma = pltpu.SemaphoreType.DMA
    square = pltpu.VMEM((D, D), BF)
    return pl.pallas_call(
        gather_kernel,
        in_specs=[hbm] * 10,
        out_specs=[vmem] * 5,
        out_shape=[
            jax.ShapeDtypeStruct((POINTS, D), BF), jax.ShapeDtypeStruct((16, D), F32), jax.ShapeDtypeStruct((POINTS + 16, D), BF),
            jax.ShapeDtypeStruct((D, A), BF), jax.ShapeDtypeStruct((A, D), BF),
        ],
        scratch_shapes=[
            pltpu.VMEM((POINTS, D), BF), square, square, square, square,
            pltpu.VMEM(point_pos.shape, BF), pltpu.VMEM(anchor_pos.shape, F32), pltpu.VMEM(send_tiles.shape, jnp.int32),
            pltpu.VMEM(nbr_slots.shape, jnp.int32), pltpu.VMEM(nbr_counts.shape, jnp.int32),
            pltpu.VMEM((128, 128), F32), pltpu.VMEM((GROUP, 16, 128), F32), pltpu.VMEM((256, POINTS), BF),
            pltpu.VMEM((GROUP, 16, D), BF), pltpu.VMEM((GROUP, 16, D), BF),
            pltpu.VMEM((3, CORES, RING, RING, RING, 16, 256), BF),
            dma((10,)), dma((15,)), dma((15,)), dma((15,)), dma((15,)),
            dma((3, 4)), dma((3, 4)), dma((3, 4)), dma((3, 4)), dma((3, 4, 4)), dma((3, 4, 4)), dma((3, 7)), dma((3, 7)),
        ],
        compiler_params=pltpu.CompilerParams(collective_id=0, has_side_effects=True, vmem_limit_bytes=28 * 2**20),
    )(*[
        pltpu.with_memory_space_constraint(operand, pltpu.HBM)
        for operand in (feats, in_weight, q_weight, k_weight, v_weight, point_pos, anchor_pos, send_tiles, nbr_slots, nbr_counts)
    ])


def block_kernel(
    emb, pooled, queries, kt, values, wo_hbm, wu_hbm, wd_hbm, anchors_hbm, points_hbm,
    wo, wu, wd, augmented, stream, finished, attended, sems, out_sems,
):
    i = pl.program_id(0)
    n = pl.num_programs(0)
    loads = [
        pltpu.make_async_copy(source, target, sems.at[k])
        for k, (source, target) in enumerate(((wo_hbm, wo), (wu_hbm, wu), (wd_hbm, wd)))
    ]

    def store(step, slot):
        return pltpu.make_async_copy(finished.at[slot], points_hbm.at[pl.ds(step * ROWS, ROWS)], out_sems.at[slot])

    @pl.when(i == 0)
    def _():
        for load in loads:
            load.start()
        low = lax.broadcasted_iota(jnp.int32, (256, 128), 1) < HD
        one = jnp.ones((256, 128), BF)
        zero = jnp.zeros((256, 128), BF)
        for c in range(0, A, 256):
            rows = slice(c, c + 256)
            for p in range(HEADS // 2):
                pair = values[rows, 128 * p:128 * p + 128]
                augmented[2 * p, rows, 0:128] = jnp.where(low, pair, zero)
                augmented[2 * p, rows, 128:256] = jnp.where(low, one, zero)
                augmented[2 * p + 1, rows, 0:128] = jnp.where(low, zero, pair)
                augmented[2 * p + 1, rows, 128:256] = jnp.where(low, zero, one)

    @pl.when(i < n - 1)
    def _():
        stream[...] = emb[pl.ds(pl.multiple_of(i * ROWS, 16), ROWS), :].astype(F32)

    @pl.when(i == n - 1)
    def _():
        stream[0:ROWS - 16, :] = emb[POINTS - (ROWS - 16):POINTS, :].astype(F32)
        stream[ROWS - 16:ROWS, :] = pooled[...]

    here = pl.ds(pl.multiple_of(i * ROWS, 16), ROWS)
    low = lax.broadcasted_iota(jnp.int32, (ROWS, 128), 1) < HD
    for p in range(HEADS // 2):
        pair = queries[here, 128 * p:128 * p + 128]
        zero = jnp.zeros_like(pair)
        out = jnp.zeros((ROWS, 256), F32)
        for a in range(2):
            query = jnp.where(low, pair, zero) if a == 0 else jnp.where(low, zero, pair)
            scores = dot(query, kt[128 * p:128 * p + 128, :])
            largest = jnp.max(scores, axis=1, keepdims=True)
            weights = jnp.exp2(scores - largest).astype(BF)
            out = out + dot(weights, augmented[2 * p + a, :, :])
        attended[:, 128 * p:128 * p + 128] = (out[:, 0:128] / out[:, 128:256]).astype(BF)

    @pl.when(i == 0)
    def _():
        for load in loads:
            load.wait()

    residual = stream[...] + dot(attended[...], wo[...])
    normed = rms(residual).astype(BF)
    result = residual
    for c in range(0, FFH, 768):
        hidden = jax.nn.gelu(dot(normed, wu[:, c:c + 768])).astype(BF)
        result = result + dot(hidden, wd[c:c + 768, :])
    slot = lax.rem(i, 2)

    @pl.when(i >= 2)
    def _():
        store(i - 2, slot).wait()

    finished[slot] = result

    @pl.when(i < n - 1)
    def _():
        store(i, slot).start()

    @pl.when(i == n - 1)
    def _():
        last = ROWS - 16
        tail = pltpu.make_async_copy(
            finished.at[slot, pl.ds(0, last)], points_hbm.at[pl.ds(POINTS - last, last)], out_sems.at[2])
        anchors = pltpu.make_async_copy(finished.at[slot, pl.ds(last, 16)], anchors_hbm, out_sems.at[3])
        tail.start()
        anchors.start()
        store(i - 1, 1 - slot).wait()
        tail.wait()
        anchors.wait()


def block(emb, pooled, queries, kt, values, out_weight, up_weight, down_weight):
    vmem = pl.BlockSpec(memory_space=pltpu.VMEM)
    hbm = pl.BlockSpec(memory_space=pltpu.HBM)
    return pl.pallas_call(
        block_kernel,
        grid=((POINTS + 16) // ROWS,),
        in_specs=[vmem] * 5 + [hbm] * 3,
        out_specs=[hbm, hbm],
        out_shape=[jax.ShapeDtypeStruct((16, D), F32), jax.ShapeDtypeStruct((POINTS, D), F32)],
        scratch_shapes=[
            pltpu.VMEM((D, D), BF), pltpu.VMEM((D, FFH), BF), pltpu.VMEM((FFH, D), BF), pltpu.VMEM((HEADS, A, 256), BF),
            pltpu.VMEM((ROWS, D), F32), pltpu.VMEM((2, ROWS, D), F32), pltpu.VMEM((ROWS, D), BF),
            pltpu.SemaphoreType.DMA((3,)), pltpu.SemaphoreType.DMA((4,)),
        ],
        compiler_params=pltpu.CompilerParams(vmem_limit_bytes=38 * 2**20, dimension_semantics=("arbitrary",)),
    )(emb, pooled, queries, kt, values, out_weight, up_weight, down_weight)


def body(point_feats, point_pos, anchor_pos, send_tiles, nbr_slots, nbr_counts, in_weight, q_weight, k_weight, v_weight,
         out_weight, up_weight, down_weight):
    emb, pooled, queries, kt, values = gather(
        point_feats.reshape(POINTS, D), in_weight, q_weight, k_weight, v_weight, jnp.transpose(point_pos, (1, 0, 2)),
        anchor_pos, send_tiles[0].T, nbr_slots.T, nbr_counts[None],
    )
    anchors, points = block(emb, pooled, queries, kt, values, out_weight, up_weight, down_weight)
    return anchors, points.reshape(POINTS // 128, 128, D)


def solution(mesh):
    both = ("blk", "pts")
    return jax.shard_map(
        body,
        mesh=mesh,
        in_specs=(P(both, None, None), P(both, None, None), P(None, both), P(both, None, None), P(both, None), P(both))
        + (P(),) * 7,
        out_specs=(P(both, None), P(both, None, None)),
        check_vma=False,
    )
```
